32 devices in a mesh: dp: 4 (over z), fsdp: 8 (over y, x, core).
Axes of the slice: x: 2, y: 2, z: 4, core: 2. Of those that a mesh axis runs over, the one named last changes fastest.
Arguments:
- frames: bfloat16 [64, 256, 1536], P(('dp', 'fsdp')), may hold values from -6 to 6
- lengths: int32 [64], P(('dp', 'fsdp')), may hold values from 1 to 256, as said below
- norm_in_gain: float32 [1536], replicated, may hold values from 0.1 to 1.9
- w_in: bfloat16 [1536, 3072], P('fsdp'), may hold values from -0.15625 to 0.15625
- dw_kernel: float32 [31, 1536], replicated, may hold values from -1 to 1
- norm_mid_gain: float32 [1536], replicated, may hold values from 0.1 to 1.9
- w_out: bfloat16 [1536, 1536], P('fsdp'), may hold values from -0.15625 to 0.15625
Outputs:
- module_out: bfloat16 [64, 256, 1536], P(('dp', 'fsdp'))
The draws below stay inside these ranges and needn't reach their ends.
Inputs may be any that keep to these rules, and one draw needn't show every extreme that they name: Utterance u has ceil(lengths[u] / 64) live blocks. Two devices of the same dp index whose fsdp indices differ by half of 8 hold at most 10 live blocks together; in every dp group some such pair holds exactly 10, one device of it having all 8 blocks live with every utterance of length 256.
All inputs are finite; a program needn't handle non-finite values.
Results may differ from the reference program's by a relative error of at most 0.0066.
Values may be sent and summed in bfloat16 or wider, within the bound.
A program may use at most 128 MiB of HBM per device.

```python
import jax
import jax.numpy as jnp
from jax import lax

D = 1536
KS = 31
BLK = 64
UB = 4
UTT_DEV = 2
FR = 256
KEEP = 5
UTTERANCES = 64
N_DP = 4
N_FSDP = 8


def draw_lengths(key, part):
    blocks_dev = UTT_DEV * UB
    half_axis = N_FSDP // 2
    devices_all = N_DP * N_FSDP
    subkeys = jax.random.split(jax.random.fold_in(key, 11), 6)
    totals = jax.random.randint(subkeys[0], (N_DP, half_axis), 2 * UTT_DEV, 2 * KEEP + 1)
    chosen = jax.random.randint(subkeys[1], (N_DP, 1), 0, half_axis)
    heavy_side = jax.random.randint(subkeys[2], (N_DP, 1), 0, 2)
    pair_pos = jnp.arange(half_axis, dtype=jnp.int32)[None, :]
    forced = pair_pos == chosen
    totals = jnp.where(forced, 2 * KEEP, totals)
    lowest = jnp.maximum(UTT_DEV, totals - blocks_dev)
    highest = jnp.minimum(blocks_dev, totals - UTT_DEV)
    first_load = jax.random.randint(subkeys[3], (N_DP, half_axis), lowest, highest + 1)
    forced_load = jnp.where(heavy_side == 0, blocks_dev, 2 * KEEP - blocks_dev)
    first_load = jnp.where(forced, forced_load, first_load)
    block_loads = jnp.concatenate([first_load, totals - first_load], axis=1).reshape(-1)
    extra_slots = UTT_DEV * (UB - 1)
    scores = jax.random.randint(subkeys[4], (devices_all, extra_slots), 0, 1 << 20) * extra_slots
    scores = scores + jnp.arange(extra_slots, dtype=jnp.int32)[None, :]
    slot_order = jnp.argsort(jnp.argsort(scores, axis=1), axis=1)
    taken_slots = (slot_order < (block_loads - UTT_DEV)[:, None]).astype(jnp.int32)
    per_utt = 1 + jnp.sum(taken_slots.reshape(devices_all, UTT_DEV, UB - 1), axis=2)
    tail_frames = jax.random.randint(subkeys[5], (devices_all, UTT_DEV), 1, BLK + 1)
    heavy_dev = jnp.arange(N_DP, dtype=jnp.int32)[:, None] * N_FSDP + chosen + heavy_side * half_axis
    dev_ids = jnp.arange(devices_all, dtype=jnp.int32)
    is_heavy = jnp.any(dev_ids[:, None] == heavy_dev.reshape(1, -1), axis=1)
    tail_frames = jnp.where(is_heavy[:, None], BLK, tail_frames)
    return ((per_utt - 1) * BLK + tail_frames).reshape(-1).astype(jnp.int32)


def steps_of(stream_key, extent, pieces, smallest, top_value):
    gain = 1.0
    for dim, shards_of in pieces:
        heights = jax.random.uniform(jax.random.fold_in(jax.random.fold_in(stream_key, 6), dim), (shards_of,), jnp.float32, smallest / len(pieces), top_value / len(pieces))
        gain = gain * jnp.repeat(jnp.exp(heights), extent[dim] // shards_of).reshape((-1,) + (1,) * (len(extent) - 1 - dim))
    return gain


def centred(rng, dims, width, most, cuts=(), held_as=jnp.bfloat16):
    array = jax.random.normal(rng, dims, jnp.float32) * width
    if len(cuts) > 0:
        array = steps_of(rng, dims, cuts, -0.22, 0.18) * array
    return jnp.clip(array, min=-most, max=most).astype(held_as)


def setup_inputs(seed: int = 0) -> dict:
    splits = jax.random.split(jax.random.key(seed), 8)
    frames = centred(splits[0], (UTTERANCES, FR, D), 1.0, 6.0, ((0, 32),))
    lengths = draw_lengths(jax.random.fold_in(splits[7], 71), 0)
    norm_in_gain = jnp.clip(1.0 + 0.18 * jax.random.normal(splits[2], (D,), jnp.float32), 0.1, 1.9)
    w_in = centred(splits[3], (D, 2 * D), D ** -0.5, 0.15625, ((0, 8),))
    dw_kernel = centred(splits[4], (KS, D), KS ** -0.5, 1.0, (), jnp.float32)
    norm_mid_gain = jnp.clip(1.0 + 0.18 * jax.random.normal(splits[5], (D,), jnp.float32), 0.1, 1.9)
    w_out = centred(splits[6], (D, D), D ** -0.5, 0.15625, ((0, 8),))
    return {"frames": frames, "lengths": lengths, "norm_in_gain": norm_in_gain, "w_in": w_in, "dw_kernel": dw_kernel, "norm_mid_gain": norm_mid_gain, "w_out": w_out}


def layer_norm(values, gain_vec):
    center = values - lax.optimization_barrier(jnp.mean(values, axis=-1, keepdims=True))
    spread = lax.optimization_barrier(jnp.mean(center * center, axis=-1, keepdims=True))
    return center * lax.rsqrt(spread + 1e-05) * gain_vec

def reference(frames, lengths, norm_in_gain, w_in, dw_kernel, norm_mid_gain, w_out):
    half_k = (KS - 1) // 2

    def one_utt(packed):
        signal, length = packed
        valid = (jnp.arange(FR, dtype=jnp.int32) < length)[:, None]
        normed = layer_norm(signal.astype(jnp.float32), norm_in_gain).astype(jnp.bfloat16)
        projected = jnp.dot(normed, w_in, preferred_element_type=jnp.float32)
        gated = jnp.where(valid, projected[:, :D] * jax.nn.sigmoid(projected[:, D:]), 0.0).astype(jnp.bfloat16)
        padded = jnp.pad(gated.astype(jnp.float32), ((half_k, half_k), (0, 0)))
        convolved = jnp.zeros((FR, D), jnp.float32)
        for offset in range(KS):
            convolved = convolved + padded[offset:offset + FR] * dw_kernel[offset]
        middle = layer_norm(convolved, norm_mid_gain)
        middle = (middle * jax.nn.sigmoid(middle)).astype(jnp.bfloat16)
        result = jnp.dot(middle, w_out, preferred_element_type=jnp.float32)
        return jnp.where(valid, result, 0.0).astype(jnp.bfloat16)
    return lax.map(one_utt, (frames, lengths))
```

```python
import jax
import jax.numpy as jnp
from jax import lax
from jax.experimental import pallas as pl
from jax.experimental.pallas import tpu as pltpu
from jax.sharding import PartitionSpec as P


def layer_norm(values, gain_vec):
    center = values - jnp.mean(values, axis=-1, keepdims=True)
    spread = jnp.mean(center * center, axis=-1, keepdims=True)
    return center * lax.rsqrt(spread + 1e-05) * gain_vec


def expand_in(flat_rows, w_in):
    model_width = flat_rows.shape[1]
    projected = jnp.dot(
        flat_rows,
        lax.all_gather(w_in, "fsdp", axis=0, tiled=True),
        preferred_element_type=jnp.float32,
    )
    return (projected[:, :model_width] * jax.nn.sigmoid(projected[:, model_width:])).astype(
        jnp.bfloat16
    )


def contract_out(flat_rows, w_out):
    projected = jnp.dot(
        flat_rows,
        lax.all_gather(w_out, "fsdp", axis=0, tiled=True),
        preferred_element_type=jnp.float32,
    )
    return projected.astype(jnp.bfloat16)


def on_device(frames, lengths, norm_in_gain, w_in, dw_kernel, norm_mid_gain, w_out):
    utt_count, frame_span, model_width = frames.shape
    positions = jnp.arange(frame_span, dtype=jnp.int32)
    valid = (positions[None, :] < lengths[:, None])[:, :, None]
    normed = layer_norm(frames.astype(jnp.float32), norm_in_gain).astype(jnp.bfloat16)

    def apply_rows(values, compute):
        return compute(values.reshape(utt_count * frame_span, model_width)).reshape(
            utt_count, frame_span, -1
        )

    def first_section(flat_rows):
        return expand_in(flat_rows, w_in)

    def last_section(flat_rows):
        return contract_out(flat_rows, w_out)

    gated = apply_rows(normed, first_section)
    gated = jnp.where(valid, gated, jnp.zeros((), jnp.bfloat16))
    taps = dw_kernel.shape[0]
    half_k = (taps - 1) // 2
    padded = jnp.pad(gated, ((0, 0), (half_k, half_k), (0, 0)))
    convolved = jnp.zeros((utt_count, frame_span, model_width), jnp.float32)
    for offset in range(taps):
        convolved = convolved + padded[:, offset : offset + frame_span, :] * dw_kernel[offset]
    middle = layer_norm(convolved, norm_mid_gain)
    middle = (middle * jax.nn.sigmoid(middle)).astype(jnp.bfloat16)
    result = apply_rows(middle, last_section)
    return jnp.where(valid, result, jnp.zeros((), jnp.bfloat16))


MESH = pl.DeviceIdType.MESH
WIDE = 512
HALO = 16
TILE = 64


def fused_kernel(
    lengths, frames, gain_in, w_in, taps, gain_mid, w_out,
    out, wbuf, normed, gated, conv, middle, load_sem, send_sem, recv_sem
):
    utts, span, width = frames.shape
    rows = w_in.shape[0]
    half = rows // 2
    cw = WIDE // 2
    n_taps = taps.shape[0]
    me = lax.axis_index("fsdp")
    dp = lax.axis_index("dp")
    par = lax.rem(dp, 2)
    core = lax.rem(me, 2)
    bit_x = lax.rem(me // 2, 2)
    bit_y = lax.rem(me // 4, 2)
    fx = me + 2 - 4 * bit_x
    fy = me + 4 - 8 * bit_y
    fxy = fx + 4 - 8 * bit_y
    fc = me + 1 - 2 * core
    to_x, to_y, to_c = {"fsdp": fx}, {"fsdp": fy}, {"fsdp": fc}
    to_z = {"dp": dp + 1 - 2 * par}
    n_in = width // cw
    n_all = n_in + width // WIDE

    def chunk(slot):
        g, r = slot // 3, slot % 3
        return 3 * g + (par if r == 0 else 1 - par if r == 1 else 2)

    def block(slot, owner, start=0, count=rows):
        first = pl.multiple_of(owner * rows + start, 16)
        return wbuf.at[chunk(slot), pl.ds(first, count), :]

    started = []

    def send(slot, kind, owner, target, start=0, count=rows):
        ref = block(slot, owner, start, count)
        copy = pltpu.make_async_remote_copy(
            src_ref=ref, dst_ref=ref,
            send_sem=send_sem.at[slot, kind], recv_sem=recv_sem.at[slot, kind],
            device_id=target, device_id_type=MESH,
        )
        copy.start()
        started.append(copy)

    def arrived(slot, kind, owner, start=0, count=rows, sem_slot=None):
        ref = block(slot, owner, start, count)
        sem = slot if sem_slot is None else sem_slot
        pltpu.make_async_remote_copy(
            src_ref=ref, dst_ref=ref,
            send_sem=send_sem.at[sem, kind], recv_sem=recv_sem.at[sem, kind],
            device_id=to_c, device_id_type=MESH,
        ).wait_recv()

    X, Y, RX, RY, C0, CX, CY, CD, ZX, ZY, ZD = range(11)

    def load_copies(slot):
        j = chunk(slot)
        own = pl.ds(pl.multiple_of(me * rows, 16), rows)
        if slot < n_in:
            lo = pl.multiple_of(j * cw, cw)
            return [
                pltpu.make_async_copy(
                    w_in.at[:, pl.ds(lo, cw)], wbuf.at[j, own, pl.ds(0, cw)],
                    load_sem.at[slot, 0]),
                pltpu.make_async_copy(
                    w_in.at[:, pl.ds(lo + width, cw)], wbuf.at[j, own, pl.ds(cw, cw)],
                    load_sem.at[slot, 1]),
            ]
        lo = pl.multiple_of((j - n_in) * WIDE, WIDE)
        return [
            pltpu.make_async_copy(
                w_out.at[:, pl.ds(lo, WIDE)], wbuf.at[j, own, :], load_sem.at[slot, 0])
        ]

    def own(slot):
        for copy in load_copies(slot):
            copy.wait()
        if slot % 3 != 1:
            send(slot, X, me, to_x)
            send(slot, Y, me, to_y)
        send(slot, C0, me, to_c)

    def relay(slot):
        arrived(slot, X, fx)
        send(slot, RY, fx, to_y, 0, half)
        if slot % 3 == 0:
            send(slot, ZX, fx, to_z)
        send(slot, CX, fx, to_c)
        arrived(slot, Y, fy)
        send(slot, RX, fy, to_x, half, half)
        if slot % 3 == 0:
            send(slot, ZY, fy, to_z)
        send(slot, CY, fy, to_c)

    def finish(slot):
        arrived(slot, RY, fxy, 0, half)
        arrived(slot, RX, fxy, half, half)
        if slot % 3 == 0:
            send(slot, ZD, fxy, to_z)
        send(slot, CD, fxy, to_c)

    def from_z(slot):
        for z_kind, c_kind, owner in ((ZX, CX, fx), (ZY, CY, fy), (ZD, CD, fxy)):
            arrived(slot, z_kind, owner, sem_slot=slot - 1)
            send(slot, c_kind, owner, to_c)

    def ready(slot):
        for kind, owner in ((C0, me), (CX, fx), (CY, fy), (CD, fxy)):
            arrived(slot, kind, owner + 1 - 2 * core)

    def norm_in():
        for u in range(utts):
            @pl.loop(0, span // TILE)
            def _(t):
                at = pl.ds(pl.multiple_of(t * TILE, TILE), TILE)
                v = frames[u, at, :].astype(jnp.float32)
                v = v - jnp.mean(v, axis=-1, keepdims=True)
                var = jnp.mean(v * v, axis=-1, keepdims=True)
                v = v * lax.rsqrt(var + 1e-05) * gain_in[...]
                normed[u, at, :] = v.astype(jnp.bfloat16)

    def project(slot):
        ready(slot)
        j = chunk(slot)
        for u in range(utts):
            acc = jnp.dot(normed[u], wbuf[j], preferred_element_type=jnp.float32)
            value = acc[:, :cw] * jax.nn.sigmoid(acc[:, cw:])
            pos = lax.broadcasted_iota(jnp.int32, (span, cw), 0)
            value = jnp.where(pos < lengths[u], value, 0.0)
            value = value.astype(jnp.bfloat16).astype(jnp.float32)
            for lane in range(cw // 128):
                gated[lane, u, HALO:HALO + span, :] = value[:, lane * 128:(lane + 1) * 128]
        for lane in range(cw // 128):
            k_at = pl.ds(pl.multiple_of(j * cw + lane * 128, 128), 128)
            for u in range(utts):
                @pl.loop(0, span // TILE)
                def _(t):
                    first = pl.multiple_of(t * TILE, TILE)
                    total = jnp.zeros((TILE, 128), jnp.float32)
                    for k in range(n_taps):
                        shift = HALO - (n_taps - 1) // 2 + k
                        total = total + gated[lane, u, pl.ds(first + shift, TILE), :] * taps[k:k + 1, k_at]
                    conv[j, u, pl.ds(first, TILE), lane * 128:(lane + 1) * 128] = total

    def norm_mid():
        for u in range(utts):
            @pl.loop(0, span // 32)
            def _(t):
                at = pl.ds(pl.multiple_of(t * 32, 32), 32)
                parts = [conv[j, u, at, :] for j in range(n_in)]
                mean = sum(jnp.sum(p, axis=-1, keepdims=True) for p in parts) / width
                parts = [p - mean for p in parts]
                var = sum(jnp.sum(p * p, axis=-1, keepdims=True) for p in parts) / width
                scale = lax.rsqrt(var + 1e-05)
                for j, p in enumerate(parts):
                    v = p * scale * gain_mid[:, j * cw:(j + 1) * cw]
                    v = v * jax.nn.sigmoid(v)
                    middle[u, at, j * cw:(j + 1) * cw] = v.astype(jnp.bfloat16)

    def contract(slot):
        ready(slot)
        j = chunk(slot)
        to = pl.ds(pl.multiple_of((j - n_in) * WIDE, WIDE), WIDE)
        for u in range(utts):
            acc = jnp.dot(middle[u], wbuf[j], preferred_element_type=jnp.float32)
            pos = lax.broadcasted_iota(jnp.int32, (span, WIDE), 0)
            out[u, :, to] = jnp.where(pos < lengths[u], acc, 0.0).astype(jnp.bfloat16)

    m0, o0, s0, m1, o1, s1, m2, o2, s2 = range(n_all)
    for slot in (m0, s0, m1, o0, s1, m2, o1, s2, o2):
        for copy in load_copies(slot):
            copy.start()
    barrier = pltpu.get_barrier_semaphore()
    for target in (to_x, to_y, to_c, to_z):
        pl.semaphore_signal(barrier, inc=1, device_id=target, device_id_type=MESH)
    pl.semaphore_wait(barrier, 4)

    own(m0)
    for lane in range(cw // 128):
        for u in range(utts):
            gated[lane, u, :HALO, :] = jnp.zeros((HALO, 128), jnp.float32)
            gated[lane, u, HALO + span:, :] = jnp.zeros((HALO, 128), jnp.float32)
    norm_in()
    relay(m0)
    own(s0)
    finish(m0)
    own(m1)
    own(o0)
    project(m0)
    relay(s0)
    own(s1)
    relay(m1)
    own(m2)
    finish(s0)
    project(s0)
    from_z(o0)
    finish(m1)
    project(o0)
    relay(s1)
    own(s2)
    own(o1)
    own(o2)
    project(m1)
    relay(m2)
    finish(s1)
    project(s1)
    from_z(o1)
    relay(s2)
    finish(m2)
    project(o1)
    finish(s2)
    norm_mid()
    contract(m2)
    contract(s2)
    from_z(o2)
    contract(o2)
    for copy in started:
        copy.wait_send()


def fused_device(frames, lengths, norm_in_gain, w_in, dw_kernel, norm_mid_gain, w_out):
    utts, span, width = frames.shape
    n_in = width // (WIDE // 2)
    n_all = n_in + width // WIDE
    vmem = pl.BlockSpec(memory_space=pltpu.VMEM)
    hbm = pl.BlockSpec(memory_space=pl.ANY)
    return pl.pallas_call(
        fused_kernel,
        out_shape=jax.ShapeDtypeStruct(frames.shape, jnp.bfloat16),
        in_specs=[pl.BlockSpec(memory_space=pltpu.SMEM), vmem, vmem, hbm, vmem, vmem, hbm],
        out_specs=vmem,
        scratch_shapes=[
            pltpu.VMEM((n_all, width, WIDE), jnp.bfloat16),
            pltpu.VMEM((utts, span, width), jnp.bfloat16),
            pltpu.VMEM((WIDE // 256, utts, span + 2 * HALO, 128), jnp.float32),
            pltpu.VMEM((n_in, utts, span, WIDE // 2), jnp.float32),
            pltpu.VMEM((utts, span, width), jnp.bfloat16),
            pltpu.SemaphoreType.DMA((n_all, 2)),
            pltpu.SemaphoreType.DMA((n_all, 11)),
            pltpu.SemaphoreType.DMA((n_all, 11)),
        ],
        compiler_params=pltpu.CompilerParams(
            collective_id=0, has_side_effects=True, vmem_limit_bytes=60000000
        ),
    )(lengths, frames, norm_in_gain.reshape(1, -1), w_in, dw_kernel,
      norm_mid_gain.reshape(1, -1), w_out)


def solution(mesh):
    paired = mesh.shape["fsdp"] == 8 and mesh.shape["dp"] % 2 == 0
    return jax.shard_map(
        fused_device if paired else on_device,
        mesh=mesh,
        in_specs=(
            P(("dp", "fsdp"), None, None),
            P(("dp", "fsdp")),
            P(),
            P("fsdp", None),
            P(),
            P(),
            P("fsdp", None),
        ),
        out_specs=P(("dp", "fsdp"), None, None),
        check_vma=False,
    )
```

```python
import jax
import jax.numpy as jnp
from jax import lax
from jax.experimental import pallas as pl
from jax.experimental.pallas import tpu as pltpu
from jax.sharding import PartitionSpec as P


def layer_norm(values, gain_vec):
    center = values - jnp.mean(values, axis=-1, keepdims=True)
    spread = jnp.mean(center * center, axis=-1, keepdims=True)
    return center * lax.rsqrt(spread + 1e-05) * gain_vec


def expand_in(flat_rows, w_in):
    model_width = flat_rows.shape[1]
    projected = jnp.dot(
        flat_rows,
        lax.all_gather(w_in, "fsdp", axis=0, tiled=True),
        preferred_element_type=jnp.float32,
    )
    return (projected[:, :model_width] * jax.nn.sigmoid(projected[:, model_width:])).astype(
        jnp.bfloat16
    )


def contract_out(flat_rows, w_out):
    projected = jnp.dot(
        flat_rows,
        lax.all_gather(w_out, "fsdp", axis=0, tiled=True),
        preferred_element_type=jnp.float32,
    )
    return projected.astype(jnp.bfloat16)


def on_device(frames, lengths, norm_in_gain, w_in, dw_kernel, norm_mid_gain, w_out):
    utt_count, frame_span, model_width = frames.shape
    positions = jnp.arange(frame_span, dtype=jnp.int32)
    valid = (positions[None, :] < lengths[:, None])[:, :, None]
    normed = layer_norm(frames.astype(jnp.float32), norm_in_gain).astype(jnp.bfloat16)

    def apply_rows(values, compute):
        return compute(values.reshape(utt_count * frame_span, model_width)).reshape(
            utt_count, frame_span, -1
        )

    def first_section(flat_rows):
        return expand_in(flat_rows, w_in)

    def last_section(flat_rows):
        return contract_out(flat_rows, w_out)

    gated = apply_rows(normed, first_section)
    gated = jnp.where(valid, gated, jnp.zeros((), jnp.bfloat16))
    taps = dw_kernel.shape[0]
    half_k = (taps - 1) // 2
    padded = jnp.pad(gated, ((0, 0), (half_k, half_k), (0, 0)))
    convolved = jnp.zeros((utt_count, frame_span, model_width), jnp.float32)
    for offset in range(taps):
        convolved = convolved + padded[:, offset : offset + frame_span, :] * dw_kernel[offset]
    middle = layer_norm(convolved, norm_mid_gain)
    middle = (middle * jax.nn.sigmoid(middle)).astype(jnp.bfloat16)
    result = apply_rows(middle, last_section)
    return jnp.where(valid, result, jnp.zeros((), jnp.bfloat16))


MESH = pl.DeviceIdType.MESH
WIDE = 512
HALO = 16
TILE = 64


def fused_kernel(
    lengths, frames, gain_in, w_in, taps, gain_mid, w_out,
    out, wbuf, normed, gated, conv, middle, load_sem, send_sem, recv_sem
):
    utts, span, width = frames.shape
    rows = w_in.shape[0]
    half = rows // 2
    cw = WIDE // 2
    n_taps = taps.shape[0]
    me = lax.axis_index("fsdp")
    dp = lax.axis_index("dp")
    par = lax.rem(dp, 2)
    core = lax.rem(me, 2)
    bit_x = lax.rem(me // 2, 2)
    bit_y = lax.rem(me // 4, 2)
    fx = me + 2 - 4 * bit_x
    fy = me + 4 - 8 * bit_y
    fxy = fx + 4 - 8 * bit_y
    fc = me + 1 - 2 * core
    to_x, to_y, to_c = {"fsdp": fx}, {"fsdp": fy}, {"fsdp": fc}
    to_z = {"dp": dp + 1 - 2 * par}
    n_in = width // cw
    n_all = n_in + width // WIDE

    def chunk(slot):
        g, r = slot // 3, slot % 3
        return 3 * g + (par if r == 0 else 1 - par if r == 1 else 2)

    def block(slot, owner, start=0, count=rows):
        first = pl.multiple_of(owner * rows + start, 16)
        return wbuf.at[chunk(slot), pl.ds(first, count), :]

    started = []

    def send(slot, kind, owner, target, start=0, count=rows):
        ref = block(slot, owner, start, count)
        copy = pltpu.make_async_remote_copy(
            src_ref=ref, dst_ref=ref,
            send_sem=send_sem.at[slot, kind], recv_sem=recv_sem.at[slot, kind],
            device_id=target, device_id_type=MESH,
        )
        copy.start()
        started.append(copy)

    def arrived(slot, kind, owner, start=0, count=rows, sem_slot=None):
        ref = block(slot, owner, start, count)
        sem = slot if sem_slot is None else sem_slot
        pltpu.make_async_remote_copy(
            src_ref=ref, dst_ref=ref,
            send_sem=send_sem.at[sem, kind], recv_sem=recv_sem.at[sem, kind],
            device_id=to_c, device_id_type=MESH,
        ).wait_recv()

    X, Y, RX, RY, C0, CX, CY, CD, ZX, ZY, ZD = range(11)

    def load_copies(slot):
        j = chunk(slot)
        own = pl.ds(pl.multiple_of(me * rows, 16), rows)
        if slot < n_in:
            lo = pl.multiple_of(j * cw, cw)
            return [
                pltpu.make_async_copy(
                    w_in.at[:, pl.ds(lo, cw)], wbuf.at[j, own, pl.ds(0, cw)],
                    load_sem.at[slot, 0]),
                pltpu.make_async_copy(
                    w_in.at[:, pl.ds(lo + width, cw)], wbuf.at[j, own, pl.ds(cw, cw)],
                    load_sem.at[slot, 1]),
            ]
        lo = pl.multiple_of((j - n_in) * WIDE, WIDE)
        return [
            pltpu.make_async_copy(
                w_out.at[:, pl.ds(lo, WIDE)], wbuf.at[j, own, :], load_sem.at[slot, 0])
        ]

    def own(slot):
        for copy in load_copies(slot):
            copy.wait()
        if slot % 3 != 1:
            send(slot, X, me, to_x)
            send(slot, Y, me, to_y)
        send(slot, C0, me, to_c)

    def relay(slot):
        arrived(slot, X, fx)
        send(slot, RY, fx, to_y, 0, half)
        if slot % 3 == 0:
            send(slot, ZX, fx, to_z)
        send(slot, CX, fx, to_c)
        arrived(slot, Y, fy)
        send(slot, RX, fy, to_x, half, half)
        if slot % 3 == 0:
            send(slot, ZY, fy, to_z)
        send(slot, CY, fy, to_c)

    def finish(slot):
        arrived(slot, RY, fxy, 0, half)
        arrived(slot, RX, fxy, half, half)
        if slot % 3 == 0:
            send(slot, ZD, fxy, to_z)
        send(slot, CD, fxy, to_c)

    def from_z(slot):
        for z_kind, c_kind, owner in ((ZX, CX, fx), (ZY, CY, fy), (ZD, CD, fxy)):
            arrived(slot, z_kind, owner, sem_slot=slot - 1)
            send(slot, c_kind, owner, to_c)

    def ready(slot):
        for kind, owner in ((C0, me), (CX, fx), (CY, fy), (CD, fxy)):
            arrived(slot, kind, owner + 1 - 2 * core)

    def norm_in():
        for u in range(utts):
            @pl.loop(0, span // TILE)
            def _(t):
                at = pl.ds(pl.multiple_of(t * TILE, TILE), TILE)
                v = frames[u, at, :].astype(jnp.float32)
                v = v - jnp.mean(v, axis=-1, keepdims=True)
                var = jnp.mean(v * v, axis=-1, keepdims=True)
                v = v * lax.rsqrt(var + 1e-05) * gain_in[...].reshape(1, width)
                normed[u, at, :] = v.astype(jnp.bfloat16)

    def project(slot):
        ready(slot)
        j = chunk(slot)
        for u in range(utts):
            acc = jnp.dot(normed[u], wbuf[j], preferred_element_type=jnp.float32)
            value = acc[:, :cw] * jax.nn.sigmoid(acc[:, cw:])
            pos = lax.broadcasted_iota(jnp.int32, (span, cw), 0)
            value = jnp.where(pos < lengths[u], value, 0.0)
            value = value.astype(jnp.bfloat16).astype(jnp.float32)
            for lane in range(cw // 128):
                gated[lane, u, HALO:HALO + span, :] = value[:, lane * 128:(lane + 1) * 128]
        for lane in range(cw // 128):
            k_at = pl.ds(pl.multiple_of(j * cw + lane * 128, 128), 128)
            for u in range(utts):
                @pl.loop(0, span // TILE)
                def _(t):
                    first = pl.multiple_of(t * TILE, TILE)
                    total = jnp.zeros((TILE, 128), jnp.float32)
                    for k in range(n_taps):
                        shift = HALO - (n_taps - 1) // 2 + k
                        total = total + gated[lane, u, pl.ds(first + shift, TILE), :] * taps[k:k + 1, k_at]
                    conv[j, u, pl.ds(first, TILE), lane * 128:(lane + 1) * 128] = total

    def norm_mid():
        for u in range(utts):
            @pl.loop(0, span // 32)
            def _(t):
                at = pl.ds(pl.multiple_of(t * 32, 32), 32)
                parts = [conv[j, u, at, :] for j in range(n_in)]
                mean = sum(jnp.sum(p, axis=-1, keepdims=True) for p in parts) / width
                parts = [p - mean for p in parts]
                var = sum(jnp.sum(p * p, axis=-1, keepdims=True) for p in parts) / width
                scale = lax.rsqrt(var + 1e-05)
                for j, p in enumerate(parts):
                    v = p * scale * gain_mid[j * cw:(j + 1) * cw].reshape(1, cw)
                    v = v * jax.nn.sigmoid(v)
                    middle[u, at, j * cw:(j + 1) * cw] = v.astype(jnp.bfloat16)

    def contract(slot):
        ready(slot)
        j = chunk(slot)
        to = pl.ds(pl.multiple_of((j - n_in) * WIDE, WIDE), WIDE)
        for u in range(utts):
            acc = jnp.dot(middle[u], wbuf[j], preferred_element_type=jnp.float32)
            out[u, :, to] = acc.astype(jnp.bfloat16)

    m0, o0, s0, m1, o1, s1, m2, o2, s2 = range(n_all)
    for slot in (m0, s0, m1, o0, s1, m2, o1, s2, o2):
        for copy in load_copies(slot):
            copy.start()
    barrier = pltpu.get_barrier_semaphore()
    for target in (to_x, to_y, to_c, to_z):
        pl.semaphore_signal(barrier, inc=1, device_id=target, device_id_type=MESH)
    pl.semaphore_wait(barrier, 4)

    own(m0)
    own(s0)
    for lane in range(cw // 128):
        for u in range(utts):
            gated[lane, u, :HALO, :] = jnp.zeros((HALO, 128), jnp.float32)
            gated[lane, u, HALO + span:, :] = jnp.zeros((HALO, 128), jnp.float32)
    norm_in()
    relay(m0)
    finish(m0)
    own(m1)
    own(o0)
    project(m0)
    relay(s0)
    own(s1)
    relay(m1)
    own(m2)
    finish(s0)
    project(s0)
    from_z(o0)
    finish(m1)
    project(o0)
    relay(s1)
    own(s2)
    own(o1)
    own(o2)
    project(m1)
    relay(m2)
    finish(s1)
    project(s1)
    from_z(o1)
    relay(s2)
    finish(m2)
    project(o1)
    finish(s2)
    norm_mid()
    contract(m2)
    contract(s2)
    from_z(o2)
    contract(o2)
    for copy in started:
        copy.wait_send()


def fused_device(frames, lengths, norm_in_gain, w_in, dw_kernel, norm_mid_gain, w_out):
    utts, span, width = frames.shape
    n_in = width // (WIDE // 2)
    n_all = n_in + width // WIDE
    vmem = pl.BlockSpec(memory_space=pltpu.VMEM)
    hbm = pl.BlockSpec(memory_space=pl.ANY)
    result = pl.pallas_call(
        fused_kernel,
        out_shape=jax.ShapeDtypeStruct(frames.shape, jnp.bfloat16),
        in_specs=[pl.BlockSpec(memory_space=pltpu.SMEM), vmem, vmem, hbm, vmem, vmem, hbm],
        out_specs=vmem,
        scratch_shapes=[
            pltpu.VMEM((n_all, width, WIDE), jnp.bfloat16),
            pltpu.VMEM((utts, span, width), jnp.bfloat16),
            pltpu.VMEM((WIDE // 256, utts, span + 2 * HALO, 128), jnp.float32),
            pltpu.VMEM((n_in, utts, span, WIDE // 2), jnp.float32),
            pltpu.VMEM((utts, span, width), jnp.bfloat16),
            pltpu.SemaphoreType.DMA((n_all, 2)),
            pltpu.SemaphoreType.DMA((n_all, 11)),
            pltpu.SemaphoreType.DMA((n_all, 11)),
        ],
        compiler_params=pltpu.CompilerParams(
            collective_id=0, has_side_effects=True, vmem_limit_bytes=60000000
        ),
    )(lengths, frames, norm_in_gain, w_in, dw_kernel,
      norm_mid_gain, w_out)
    valid = jnp.arange(span, dtype=jnp.int32)[None, :] < lengths[:, None]
    return jnp.where(valid[:, :, None], result, jnp.zeros((), jnp.bfloat16))


def solution(mesh):
    paired = mesh.shape["fsdp"] == 8 and mesh.shape["dp"] % 2 == 0
    return jax.shard_map(
        fused_device if paired else on_device,
        mesh=mesh,
        in_specs=(
            P(("dp", "fsdp"), None, None),
            P(("dp", "fsdp")),
            P(),
            P("fsdp", None),
            P(),
            P(),
            P("fsdp", None),
        ),
        out_specs=P(("dp", "fsdp"), None, None),
        check_vma=False,
    )
```
